32 devices in a mesh: dp: 8 (over z, x), tp: 4 (over y, core).
Axes of the slice: x: 2, y: 2, z: 4, core: 2. Of those that a mesh axis runs over, the one named last changes fastest.
Arguments:
- activations: bfloat16 [2048, 4096], P('dp'), may hold values from -6 to 6
- out_grads: bfloat16 [2048, 4096], P('dp', 'tp'), may hold values from -6 to 6
- residual: bfloat16 [32768, 4096], P('dp', 'tp'), may hold values from -24 to 24
- right_prev: bfloat16 [4096, 32], P('tp'), may hold values from -6 to 6
Outputs:
- update: bfloat16 [4096, 4096], P(None, 'tp')
- left_basis: float32 [4096, 32], replicated
- right_factor: float32 [4096, 32], P('tp')
The draws below stay inside these ranges and needn't reach their ends.
All inputs are finite; a program needn't handle non-finite values.
Results may differ from the reference program's by a relative error of at most 0.0061.
Values sent between devices are 32-bit elements; how exact they have to be, the bound alone decides.
A program may use at most 64 MiB of HBM per device.

```python
import jax
import jax.numpy as jnp
from jax import lax

D = 4096
QD = 4096
RANK = 32
TOK_DEV = 256
TOKENS = 2048
N_DP = 8


def level_of(stream_key, extent, cuts, smallest, top_value):
    def one(dim, shards_of):
        heights = jax.random.uniform(jax.random.fold_in(jax.random.fold_in(stream_key, 6), dim), (shards_of,), jnp.float32, smallest / len(cuts), top_value / len(cuts))
        return jnp.repeat(jnp.exp(heights), extent[dim] // shards_of).reshape((-1,) + (1,) * (len(extent) - dim - 1))

    gain = one(*cuts[0])
    for cut in cuts[1:]:
        gain = gain * one(*cut)
    return gain


def centred(rng, shape, spread, limit, cuts=(), dtype=jnp.bfloat16):
    result = jax.random.normal(rng, shape, jnp.float32) * spread
    if len(cuts) > 0:
        result = level_of(rng, shape, cuts, -0.22, 0.18) * result
    return jnp.clip(result, min=-limit, max=limit).astype(dtype)


def setup_inputs(seed: int = 0) -> dict:
    key_list = jax.random.split(jax.random.key(seed), 5)
    activations = centred(key_list[0], (TOKENS, D), 1.0, 6.0, ((0, 8),))
    out_grads = centred(key_list[1], (TOKENS, QD), 0.5, 6.0, ((0, 8), (1, 4)))
    residual = centred(key_list[2], (N_DP * D, QD), 4.0, 24.0, ((0, 8), (1, 4)))
    right_prev = centred(key_list[3], (QD, RANK), 1.0, 6.0, ((0, 4),))
    return dict(activations=activations, out_grads=out_grads, residual=residual, right_prev=right_prev)


def reference(activations, out_grads, residual, right_prev):
    activ_blocks = activations.reshape(N_DP, TOK_DEV, D)
    grad_blocks = out_grads.reshape(N_DP, TOK_DEV, QD)
    resid_blocks = residual.reshape(N_DP, D, QD)

    def advance(running, pieces):
        activ_piece, grad_piece, resid_piece = pieces
        product = lax.dot_general(activ_piece.astype(jnp.float32), grad_piece.astype(jnp.float32), (((0,), (0,)), ((), ())), preferred_element_type=jnp.float32)
        merged = (product + resid_piece.astype(jnp.float32)).astype(jnp.bfloat16)
        return (running + merged.astype(jnp.float32), None)
    merged_total, _ = lax.scan(advance, jnp.zeros((D, QD), jnp.float32), (activ_blocks, grad_blocks, resid_blocks))
    left_sum = jnp.dot(merged_total, right_prev.astype(jnp.float32), precision=lax.Precision.HIGHEST)
    gram_matrix = jnp.dot(left_sum.T, left_sum, precision=lax.Precision.HIGHEST)
    lower_factor = jnp.linalg.cholesky(gram_matrix)
    left_basis = lax.linalg.triangular_solve(lower_factor, left_sum, left_side=False, lower=True, transpose_a=True)
    left_half = lax.optimization_barrier(left_basis.astype(jnp.bfloat16)).astype(jnp.float32)
    right_factor = jnp.dot(merged_total.T, left_half, precision=lax.Precision.HIGHEST) / N_DP
    update = jnp.dot(left_basis, right_factor.T, precision=lax.Precision.HIGHEST).astype(jnp.bfloat16)
    return (update, left_basis, right_factor)
```

```python
import functools
import itertools

import jax
import jax.numpy as jnp
from jax import lax
from jax.experimental import pallas as pl
from jax.experimental.pallas import tpu as pltpu
from jax.sharding import PartitionSpec as P

LANES = 128
HIGHEST = lax.Precision.HIGHEST


def plain_shards(activations, out_grads, residual, right_prev):
    product = lax.dot_general(
        activations, out_grads, (((0,), (0,)), ((), ())), preferred_element_type=jnp.float32
    )
    merged = (product + residual.astype(jnp.float32)).astype(jnp.bfloat16)
    shard_sum = lax.psum_scatter(
        jnp.dot(merged, right_prev, preferred_element_type=jnp.float32),
        "tp",
        scatter_dimension=0,
        tiled=True,
    )
    block_sum = lax.psum(shard_sum, "dp")
    block_gram = jnp.dot(block_sum.T, block_sum, precision=HIGHEST)
    gram_matrix = lax.psum(block_gram, "tp")
    lower_factor = jnp.linalg.cholesky(gram_matrix)
    basis_block = lax.linalg.triangular_solve(
        lower_factor, block_sum, left_side=False, lower=True, transpose_a=True
    )
    left_basis = lax.all_gather(basis_block, "tp", axis=0, tiled=True)
    left_half = left_basis.astype(jnp.bfloat16)
    coeff_terms = lax.dot_general(
        merged, left_half, (((0,), (0,)), ((), ())), preferred_element_type=jnp.float32
    )
    right_factor = lax.psum(coeff_terms, "dp") / lax.axis_size("dp")
    update = jnp.dot(left_basis, right_factor.T, precision=HIGHEST).astype(jnp.bfloat16)
    return (update, left_basis, right_factor)


def digits_of(axis, size):
    if size == 1:
        return []
    if size % 2 == 0 and size > 2:
        return [(axis, 1, 2), (axis, 2, size // 2)]
    return [(axis, 1, size)]


def members(stage):
    count = 1
    for _, _, size in stage:
        count *= size
    return count


def offsets(stage):
    return list(itertools.product(*[range(size) for _, _, size in stage]))[1:]


def member_index(stage, place):
    index = 0
    for axis, stride, size in stage:
        index = index * size + (place[axis] // stride) % size
    return index


def moved(stage, offset, place, sign=1):
    there = dict(place)
    for (axis, stride, size), step in zip(stage, offset):
        digit = (place[axis] // stride) % size
        there[axis] = there[axis] + (((digit + sign * step + size) % size) - digit) * stride
    return there


def round_kernel(
    left_stages, right_stages, n_chunk, axes,
    act, grads, resid, right_prev, basis_out, coeff_out,
    xbuf, ybuf, merged, acc, full, acc2, full2, *rest,
):
    n_left = len(left_stages)
    left_recv = rest[:n_left]
    right_recv = rest[n_left : n_left + len(right_stages)]
    in_sem, send_sem, recv_sem = rest[n_left + len(right_stages) :]
    place = {axis: lax.axis_index(axis) for axis in axes}
    barrier = pltpu.get_barrier_semaphore()
    peers = {}
    for stage in left_stages + right_stages:
        for offset in offsets(stage):
            key = tuple(sorted((d, s) for d, s in zip(stage, offset) if s))
            peers[key] = moved(stage, offset, place)
    for peer in peers.values():
        pl.semaphore_signal(barrier, inc=1, device_id=peer, device_id_type=pl.DeviceIdType.MESH)

    rows = resid.shape[0]
    chunk = rows // n_chunk
    per = chunk // LANES
    width = acc.shape[1]

    def x_copy(c):
        at = pl.multiple_of(c * chunk, chunk)
        return pltpu.make_async_copy(act.at[:, pl.ds(at, chunk)], xbuf.at[c], in_sem.at[c])

    def e_copy(c):
        at = pl.multiple_of(c * chunk, chunk)
        return pltpu.make_async_copy(
            resid.at[pl.ds(at, chunk), :], merged.at[pl.ds(at, chunk), :], in_sem.at[n_chunk + c]
        )

    y_copy = pltpu.make_async_copy(grads, ybuf, in_sem.at[2 * n_chunk])
    y_copy.start()
    for c in range(n_chunk):
        x_copy(c).start()
        e_copy(c).start()
    y_copy.wait()

    def merge(c, carry):
        x_copy(c).wait()
        e_copy(c).wait()
        at = pl.multiple_of(c * chunk, chunk)
        product = lax.dot_general(
            xbuf[c], ybuf[...], (((0,), (0,)), ((), ())), preferred_element_type=jnp.float32
        )
        piece = (product + merged[pl.ds(at, chunk), :].astype(jnp.float32)).astype(jnp.bfloat16)
        merged[pl.ds(at, chunk), :] = piece
        term = lax.dot_general(
            right_prev[...], piece, (((1,), (1,)), ((), ())), preferred_element_type=jnp.float32
        )
        for b in range(per):
            acc[c * per + b] = term[:, b * LANES : (b + 1) * LANES]
        return carry

    lax.fori_loop(0, n_chunk, merge, 0)
    pl.semaphore_wait(barrier, len(peers))

    slot = [0]

    def remote(src, dst, peer):
        n = slot[0]
        slot[0] += 1
        return pltpu.make_async_remote_copy(
            src_ref=src, dst_ref=dst, send_sem=send_sem.at[n], recv_sem=recv_sem.at[n],
            device_id=peer, device_id_type=pl.DeviceIdType.MESH,
        )

    def all_reduce(stages, acc_ref, recv_refs, full_ref):
        lo, count = 0, acc_ref.shape[0]
        held, sent = [], []
        for stage, recv in zip(stages, recv_refs):
            size = count // members(stage)
            copies = []
            for k, offset in enumerate(offsets(stage)):
                peer = moved(stage, offset, place)
                start = lo + member_index(stage, peer) * size
                copies.append(remote(acc_ref.at[pl.ds(start, size)], recv.at[k], peer))
                copies[-1].start()
            held.append((lo, count))
            lo, count = lo + member_index(stage, place) * size, size
            total = acc_ref[pl.ds(lo, count)]
            for k, copy in enumerate(copies):
                copy.wait_recv()
                total = total + recv[k]
            sent += copies
            if stage is stages[-1]:
                full_ref[pl.ds(lo, count)] = total
            else:
                acc_ref[pl.ds(lo, count)] = total
        for stage, (outer, outer_count) in zip(reversed(stages), reversed(held)):
            copies = []
            for offset in offsets(stage):
                peer = moved(stage, offset, place)
                mine = full_ref.at[pl.ds(lo, count)]
                copies.append(remote(mine, mine, peer))
                copies[-1].start()
            for copy in copies:
                copy.wait_recv()
            sent += copies
            lo, count = outer, outer_count
        return sent

    sent = all_reduce(left_stages, acc, left_recv, full)
    left_sum = jnp.concatenate([full[b] for b in range(full.shape[0])], axis=1)
    gram = lax.dot_general(
        left_sum, left_sum, (((1,), (1,)), ((), ())),
        precision=HIGHEST, preferred_element_type=jnp.float32,
    )
    row_id = lax.broadcasted_iota(jnp.int32, (width, LANES), 0)
    col_id = lax.broadcasted_iota(jnp.int32, (width, LANES), 1)
    work = jnp.concatenate(
        [gram, (row_id + width == col_id).astype(jnp.float32)[:, width:]], axis=1
    )
    for j in range(width):
        column = jnp.broadcast_to(work[:, j : j + 1], (width, LANES))
        scaled = work[j : j + 1, :] / column[j : j + 1, :]
        work = work - jnp.where(row_id > j, column, 0.0) * scaled
    pivots = jnp.sum(jnp.where(row_id == col_id, work, 0.0), axis=1, keepdims=True)
    inverse = work[:, width : 2 * width] / jnp.sqrt(pivots)
    basis = jnp.dot(inverse, left_sum, precision=HIGHEST, preferred_element_type=jnp.float32)
    basis_out[...] = basis
    half = basis.astype(jnp.bfloat16)
    columns = merged.shape[1]
    tile = 2 * LANES

    def terms(j, carry):
        at = pl.multiple_of(j * tile, tile)
        part = jnp.dot(half, merged[:, pl.ds(at, tile)], preferred_element_type=jnp.float32)
        acc2[2 * j] = part[:, :LANES]
        acc2[2 * j + 1] = part[:, LANES:]
        return carry

    lax.fori_loop(0, columns // tile, terms, 0)
    sent += all_reduce(right_stages, acc2, right_recv, full2)
    scale = 1.0 / members(right_stages[0])
    for b in range(full2.shape[0]):
        coeff_out[:, b * LANES : (b + 1) * LANES] = full2[b] * scale
    for copy in sent:
        copy.wait_send()


def split(value):
    high = value.astype(jnp.bfloat16)
    return high, (value - high.astype(jnp.float32)).astype(jnp.bfloat16)


def update_kernel(basis, coeff, update_out, basis_out, coeff_out):
    left_high, left_low = split(basis[...])
    right_high, right_low = split(coeff[...])
    left = jnp.concatenate([left_high, left_low, left_high], axis=0)
    right = jnp.concatenate([right_high, right_high, right_low], axis=0)
    update_out[...] = lax.dot_general(
        left, right, (((0,), (0,)), ((), ())), preferred_element_type=jnp.float32
    ).astype(jnp.bfloat16)
    basis_out[...] = basis[...]
    coeff_out[...] = coeff[...]


def fast_shards(axes, sizes, activations, out_grads, residual, right_prev):
    rows, columns = residual.shape
    tokens = activations.shape[0]
    rank = right_prev.shape[1]
    n_dp, n_tp = sizes["dp"], sizes["tp"]
    tp_digits, dp_digits = digits_of("tp", n_tp), digits_of("dp", n_dp)
    left_stages = [s for s in (tp_digits[:1], tp_digits[1:] + dp_digits[:1], dp_digits[1:]) if s]
    right_stages = [dp_digits]
    n_chunk = max(1, rows // 512)
    blocks, blocks2 = rows // LANES, columns // LANES

    def recv_shapes(stages, count):
        shapes = []
        for stage in stages:
            count //= members(stage)
            shapes.append(pltpu.VMEM((members(stage) - 1, count, rank, LANES), jnp.float32))
        return shapes

    n_copies = 2 * sum(members(s) - 1 for s in left_stages + right_stages)
    vmem = pl.BlockSpec(memory_space=pltpu.VMEM)
    hbm = pl.BlockSpec(memory_space=pl.ANY)
    basis, coeff = pl.pallas_call(
        functools.partial(round_kernel, left_stages, right_stages, n_chunk, axes),
        out_shape=(
            jax.ShapeDtypeStruct((rank, rows), jnp.float32),
            jax.ShapeDtypeStruct((rank, columns), jnp.float32),
        ),
        in_specs=[hbm, hbm, hbm, vmem],
        out_specs=(vmem, vmem),
        scratch_shapes=[
            pltpu.VMEM((n_chunk, tokens, rows // n_chunk), jnp.bfloat16),
            pltpu.VMEM((tokens, columns), jnp.bfloat16),
            pltpu.VMEM((rows, columns), jnp.bfloat16),
            pltpu.VMEM((blocks, rank, LANES), jnp.float32),
            pltpu.VMEM((blocks, rank, LANES), jnp.float32),
            pltpu.VMEM((blocks2, rank, LANES), jnp.float32),
            pltpu.VMEM((blocks2, rank, LANES), jnp.float32),
            *recv_shapes(left_stages, blocks),
            *recv_shapes(right_stages, blocks2),
            pltpu.SemaphoreType.DMA((2 * n_chunk + 1,)),
            pltpu.SemaphoreType.DMA((n_copies,)),
            pltpu.SemaphoreType.DMA((n_copies,)),
        ],
        compiler_params=pltpu.CompilerParams(
            collective_id=0, has_side_effects=True, vmem_limit_bytes=40 * 2**20
        ),
        name="powersgd_round",
    )(activations, out_grads, residual, right_prev.T)
    step = min(rows, 512)
    update, basis, coeff = pl.pallas_call(
        update_kernel,
        grid=(rows // step,),
        out_shape=(
            jax.ShapeDtypeStruct((rows, columns), jnp.bfloat16),
            jax.ShapeDtypeStruct((rank, rows), jnp.float32),
            jax.ShapeDtypeStruct((rank, columns), jnp.float32),
        ),
        in_specs=[
            pl.BlockSpec((rank, step), lambda i: (0, i)),
            pl.BlockSpec((rank, columns), lambda i: (0, 0)),
        ],
        out_specs=(
            pl.BlockSpec((step, columns), lambda i: (i, 0)),
            pl.BlockSpec((rank, step), lambda i: (0, i)),
            pl.BlockSpec((rank, columns), lambda i: (0, 0)),
        ),
        compiler_params=pltpu.CompilerParams(vmem_limit_bytes=16 * 2**20),
        name="powersgd_update",
    )(basis, coeff)
    return update, basis.T, coeff.T


def shards(axes, sizes, activations, out_grads, residual, right_prev):
    rows, columns = residual.shape
    n_dp, n_tp = sizes["dp"], sizes["tp"]
    fits = (
        rows % (LANES * n_dp * n_tp) == 0
        and rows % 512 == 0
        and columns % (2 * LANES) == 0
        and columns % (LANES * n_dp) == 0
        and right_prev.shape[1] * 2 <= LANES
        and n_dp > 1
    )
    if not fits:
        return plain_shards(activations, out_grads, residual, right_prev)
    return fast_shards(axes, sizes, activations, out_grads, residual, right_prev)


def solution(mesh):
    in_specs = (P("dp", None), P("dp", "tp"), P("dp", "tp"), P("tp", None))
    out_specs = (P(None, "tp"), P(), P("tp", None))
    body = functools.partial(shards, mesh.axis_names, dict(mesh.shape))
    return jax.shard_map(body, mesh=mesh, in_specs=in_specs, out_specs=out_specs, check_vma=False)
```

```python
import functools
import itertools

import jax
import jax.numpy as jnp
from jax import lax
from jax.experimental import pallas as pl
from jax.experimental.pallas import tpu as pltpu
from jax.sharding import PartitionSpec as P

LANES = 128
ROWS = 8
HIGHEST = lax.Precision.HIGHEST


def plain_shards(activations, out_grads, residual, right_prev):
    product = lax.dot_general(
        activations, out_grads, (((0,), (0,)), ((), ())), preferred_element_type=jnp.float32
    )
    merged = (product + residual.astype(jnp.float32)).astype(jnp.bfloat16)
    shard_sum = lax.psum_scatter(
        jnp.dot(merged, right_prev, preferred_element_type=jnp.float32),
        "tp",
        scatter_dimension=0,
        tiled=True,
    )
    block_sum = lax.psum(shard_sum, "dp")
    block_gram = jnp.dot(block_sum.T, block_sum, precision=HIGHEST)
    gram_matrix = lax.psum(block_gram, "tp")
    lower_factor = jnp.linalg.cholesky(gram_matrix)
    basis_block = lax.linalg.triangular_solve(
        lower_factor, block_sum, left_side=False, lower=True, transpose_a=True
    )
    left_basis = lax.all_gather(basis_block, "tp", axis=0, tiled=True)
    left_half = left_basis.astype(jnp.bfloat16)
    coeff_terms = lax.dot_general(
        merged, left_half, (((0,), (0,)), ((), ())), preferred_element_type=jnp.float32
    )
    right_factor = lax.psum(coeff_terms, "dp") / lax.axis_size("dp")
    update = jnp.dot(left_basis, right_factor.T, precision=HIGHEST).astype(jnp.bfloat16)
    return (update, left_basis, right_factor)


def digits_of(axis, size):
    if size == 1:
        return []
    if size % 2 == 0 and size > 2:
        return [(axis, 1, 2), (axis, 2, size // 2)]
    return [(axis, 1, size)]


def members(stage):
    count = 1
    for _, _, size in stage:
        count *= size
    return count


def offsets(stage):
    return list(itertools.product(*[range(size) for _, _, size in stage]))[1:]


def member_index(stage, place):
    index = 0
    for axis, stride, size in stage:
        index = index * size + (place[axis] // stride) % size
    return index


def moved(stage, offset, place, sign=1):
    there = dict(place)
    for (axis, stride, size), step in zip(stage, offset):
        digit = (place[axis] // stride) % size
        there[axis] = there[axis] + (((digit + sign * step + size) % size) - digit) * stride
    return there


def split(value):
    high = value.astype(jnp.bfloat16)
    return high, (value - high.astype(jnp.float32)).astype(jnp.bfloat16)


def joined(units, rank):
    tall = rank // ROWS
    n = units.shape[0] // tall
    bands = [
        jnp.concatenate([units[b * tall + r] for b in range(n)], axis=1) for r in range(tall)
    ]
    return jnp.concatenate(bands, axis=0)


def round_kernel(
    left_stages, right_stages, n_chunk, axes,
    act, grads, resid, right_prev, basis_out, coeff_out,
    xbuf, ybuf, rbuf, merged, terms, acc2, full2, *rest,
):
    rest = list(rest)
    in_sem, send_sem, recv_sem = rest[-3:]
    take = iter(rest[:-3])
    acc, full = next(take), next(take)
    left_recv = [next(take) for _ in left_stages]
    right_recv = [next(take) for _ in right_stages]
    place = {axis: lax.axis_index(axis) for axis in axes}
    barrier = pltpu.get_barrier_semaphore()
    peers = {}
    for stage in left_stages + right_stages:
        for offset in offsets(stage):
            key = tuple(sorted((d, s) for d, s in zip(stage, offset) if s))
            peers[key] = moved(stage, offset, place)
    for peer in peers.values():
        pl.semaphore_signal(barrier, inc=1, device_id=peer, device_id_type=pl.DeviceIdType.MESH)

    rows, columns = resid.shape
    rank = right_prev.shape[0]
    tall = rank // ROWS
    chunk = rows // n_chunk
    per = chunk // LANES
    units = per * tall
    first, second = left_stages[:2]
    n0, n1 = members(first), members(second)
    order = []
    for offset in offsets(first) + [(0,) * len(first)]:
        for offset2 in offsets(second) + [(0,) * len(second)]:
            there = moved(second, offset2, moved(first, offset, place))
            order.append(member_index(first, there) * n1 + member_index(second, there))

    def x_copy(c):
        at = pl.multiple_of(c * chunk, chunk)
        return pltpu.make_async_copy(act.at[:, pl.ds(at, chunk)], xbuf.at[c], in_sem.at[c])

    def e_copy(c):
        at = pl.multiple_of(c * chunk, chunk)
        return pltpu.make_async_copy(
            resid.at[pl.ds(at, chunk), :], merged.at[pl.ds(at, chunk), :], in_sem.at[n_chunk + c]
        )

    y_copy = pltpu.make_async_copy(grads, ybuf, in_sem.at[2 * n_chunk])
    r_copy = pltpu.make_async_copy(right_prev, rbuf, in_sem.at[2 * n_chunk + 1])
    y_copy.start()
    r_copy.start()
    for c in order:
        x_copy(c).start()
        e_copy(c).start()
    y_copy.wait()
    r_copy.wait()

    slot = [0]
    sent = []

    def remote(src, dst, peer):
        n = slot[0]
        slot[0] += 1
        copy = pltpu.make_async_remote_copy(
            src_ref=src, dst_ref=dst, send_sem=send_sem.at[n], recv_sem=recv_sem.at[n],
            device_id=peer, device_id_type=pl.DeviceIdType.MESH,
        )
        copy.start()
        sent.append(copy)
        return copy

    def all_reduce(stages, acc_ref, recv_refs, full_ref, lo, count, held):
        for stage, recv in zip(stages, recv_refs):
            size = count // members(stage)
            copies = []
            for k, offset in enumerate(offsets(stage)):
                peer = moved(stage, offset, place)
                start = lo + member_index(stage, peer) * size
                copies.append(remote(acc_ref.at[pl.ds(start, size)], recv.at[k], peer))
            held = held + [(stage, lo, count)]
            lo, count = lo + member_index(stage, place) * size, size
            yield
            total = acc_ref[pl.ds(lo, count)]
            for k, copy in enumerate(copies):
                copy.wait_recv()
                total = total + recv[k]
            if stage is stages[-1]:
                full_ref[pl.ds(lo, count)] = total
            else:
                acc_ref[pl.ds(lo, count)] = total
        for stage, outer, outer_count in reversed(held):
            copies = []
            for offset in offsets(stage):
                peer = moved(stage, offset, place)
                mine = full_ref.at[pl.ds(lo, count)]
                copies.append(remote(mine, mine, peer))
            yield
            for copy in copies:
                copy.wait_recv()
            lo, count = outer, outer_count

    def advance(flow):
        return next(flow, "done") != "done"

    def merge(c):
        x_copy(c).wait()
        e_copy(c).wait()
        at = pl.multiple_of(c * chunk, chunk)
        product = lax.dot_general(
            xbuf[c], ybuf[...], (((0,), (0,)), ((), ())), preferred_element_type=jnp.float32
        )
        piece = (product + merged[pl.ds(at, chunk), :].astype(jnp.float32)).astype(jnp.bfloat16)
        merged[pl.ds(at, chunk), :] = piece
        term = lax.dot_general(
            rbuf[...], piece, (((1,), (1,)), ((), ())), preferred_element_type=jnp.float32
        )
        return [
            term[r * ROWS : (r + 1) * ROWS, b * LANES : (b + 1) * LANES]
            for b in range(per) for r in range(tall)
        ]

    arrivals = {}
    second_copies = []
    for n, c in enumerate(order):
        k0, k1 = divmod(n, n1)
        terms_of_chunk = merge(c)
        at = c * units
        if n == 0:
            pl.semaphore_wait(barrier, len(peers))
        if k0 < n0 - 1:
            for u, term in enumerate(terms_of_chunk):
                acc[at + u] = term
            peer = moved(first, offsets(first)[k0], place)
            arrivals[k0, k1] = remote(acc.at[pl.ds(at, units)], left_recv[0].at[k0, k1], peer)
            continue
        for j in range(n0 - 1):
            arrivals[j, k1].wait_recv()
        for u, term in enumerate(terms_of_chunk):
            for j in range(n0 - 1):
                term = term + left_recv[0][j, k1, u]
            acc[at + u] = term
        if k1 < n1 - 1:
            peer = moved(second, offsets(second)[k1], place)
            second_copies.append(remote(acc.at[pl.ds(at, units)], left_recv[1].at[k1], peer))
    mine = order[-1] * units
    total = acc[pl.ds(mine, units)]
    for k, copy in enumerate(second_copies):
        copy.wait_recv()
        total = total + left_recv[1][k]
    acc[pl.ds(mine, units)] = total

    tile = 2 * LANES
    span = rows // n0

    def add_terms(index, step):
        at = pl.multiple_of(index * span, span)
        both = jnp.concatenate(
            split(joined(full[pl.ds(index * n1 * units, n1 * units)], rank)), axis=0
        )

        def column_tile(j, carry):
            col = pl.multiple_of(j * tile, tile)
            part = jnp.dot(
                both, merged[pl.ds(at, span), pl.ds(col, tile)],
                preferred_element_type=jnp.float32,
            )
            part = part[:rank] + part[rank:]
            if step > 0:
                part = part + terms[:, pl.ds(col, tile)]
            if step < n0 - 1:
                terms[:, pl.ds(col, tile)] = part
            else:
                for b in range(2):
                    for r in range(tall):
                        acc2[(2 * j + b) * tall + r] = part[
                            r * ROWS : (r + 1) * ROWS, b * LANES : (b + 1) * LANES
                        ]
            return carry

        lax.fori_loop(0, columns // tile, column_tile, 0)

    flow = all_reduce(
        left_stages[2:], acc, left_recv[2:], full, mine, units,
        [(first, 0, n_chunk * units), (second, member_index(first, place) * n1 * units, n1 * units)],
    )
    for _ in range(2 * len(left_stages[2:]) + 2):
        advance(flow)
    add_terms(member_index(first, place), 0)
    while advance(flow):
        pass
    for k, offset in enumerate(offsets(first)):
        add_terms(member_index(first, moved(first, offset, place)), k + 1)

    right_flow = all_reduce(right_stages, acc2, right_recv, full2, 0, acc2.shape[0], [])
    advance(right_flow)
    left_sum = joined(full[...], rank)
    gram = lax.dot_general(
        left_sum, left_sum, (((1,), (1,)), ((), ())),
        precision=HIGHEST, preferred_element_type=jnp.float32,
    )
    row_id = lax.broadcasted_iota(jnp.int32, (rank, LANES), 0)
    col_id = lax.broadcasted_iota(jnp.int32, (rank, LANES), 1)
    work = jnp.concatenate(
        [gram, (row_id + rank == col_id).astype(jnp.float32)[:, rank:]], axis=1
    )
    for j in range(rank):
        column = jnp.broadcast_to(work[:, j : j + 1], (rank, LANES))
        scaled = work[j : j + 1, :] / column[j : j + 1, :]
        work = work - jnp.where(row_id > j, column, 0.0) * scaled
    pivots = jnp.sum(jnp.where(row_id == col_id, work, 0.0), axis=1, keepdims=True)
    inverse = work[:, rank : 2 * rank] / jnp.sqrt(pivots)
    advance(right_flow)
    basis_out[...] = jnp.dot(
        inverse, left_sum, precision=HIGHEST, preferred_element_type=jnp.float32
    )
    while advance(right_flow):
        pass
    coeff_out[...] = jnp.dot(
        inverse * (1.0 / lax.axis_size("dp")), joined(full2[...], rank),
        precision=HIGHEST, preferred_element_type=jnp.float32,
    )
    for copy in sent:
        copy.wait_send()


def update_kernel(basis, coeff, update_out, basis_out, coeff_out):
    left_high, left_low = split(basis[...])
    right_high, right_low = split(coeff[...])
    left = jnp.concatenate([left_high, left_low, left_high], axis=0)
    right = jnp.concatenate([right_high, right_high, right_low], axis=0)
    update_out[...] = lax.dot_general(
        left, right, (((0,), (0,)), ((), ())), preferred_element_type=jnp.float32
    ).astype(jnp.bfloat16)
    basis_out[...] = basis[...]
    coeff_out[...] = coeff[...]


def fast_shards(axes, sizes, activations, out_grads, residual, right_prev):
    rows, columns = residual.shape
    tokens = activations.shape[0]
    rank = right_prev.shape[1]
    n_dp, n_tp = sizes["dp"], sizes["tp"]
    tp_digits, dp_digits = digits_of("tp", n_tp), digits_of("dp", n_dp)
    left_stages = [s for s in (tp_digits[:1], tp_digits[1:] + dp_digits[:1], dp_digits[1:]) if s]
    right_stages = [dp_digits]
    n_first, n_second = members(left_stages[0]), members(left_stages[1])
    n_chunk = n_first * n_second
    tall = rank // ROWS
    units, units2 = rows // LANES * tall, columns // LANES * tall

    def unit_buffer(*lead):
        return pltpu.VMEM((*lead, ROWS, LANES), jnp.float32)

    def recv_buffers(stages, count):
        buffers = []
        for stage in stages:
            count //= members(stage)
            buffers.append(unit_buffer(members(stage) - 1, count))
        return buffers

    n_copies = 2 * sum(members(s) - 1 for s in right_stages + left_stages[1:])
    n_copies += (n_first - 1) * (n_second + 1)
    vmem = pl.BlockSpec(memory_space=pltpu.VMEM)
    hbm = pl.BlockSpec(memory_space=pltpu.HBM)
    basis, coeff = pl.pallas_call(
        functools.partial(round_kernel, left_stages, right_stages, n_chunk, axes),
        out_shape=(
            jax.ShapeDtypeStruct((rank, rows), jnp.float32),
            jax.ShapeDtypeStruct((rank, columns), jnp.float32),
        ),
        in_specs=[hbm, hbm, hbm, hbm],
        out_specs=(vmem, vmem),
        scratch_shapes=[
            pltpu.VMEM((n_chunk, tokens, rows // n_chunk), jnp.bfloat16),
            pltpu.VMEM((tokens, columns), jnp.bfloat16),
            pltpu.VMEM((rank, columns), jnp.bfloat16),
            pltpu.VMEM((rows, columns), jnp.bfloat16),
            pltpu.VMEM((rank, columns), jnp.float32),
            unit_buffer(units2),
            unit_buffer(units2),
            unit_buffer(units),
            unit_buffer(units),
            unit_buffer(n_first - 1, n_second, units // n_chunk),
            *recv_buffers(left_stages[1:], units // n_first),
            *recv_buffers(right_stages, units2),
            pltpu.SemaphoreType.DMA((2 * n_chunk + 2,)),
            pltpu.SemaphoreType.DMA((n_copies,)),
            pltpu.SemaphoreType.DMA((n_copies,)),
        ],
        compiler_params=pltpu.CompilerParams(
            collective_id=0, has_side_effects=True, vmem_limit_bytes=63 * 2**20 + 512 * 2**10
        ),
        name="powersgd_round",
    )(activations, out_grads, residual, right_prev.T)
    step = rows // 4
    update, basis, coeff = pl.pallas_call(
        update_kernel,
        grid=(rows // step,),
        out_shape=(
            jax.ShapeDtypeStruct((rows, columns), jnp.bfloat16),
            jax.ShapeDtypeStruct((rank, rows), jnp.float32),
            jax.ShapeDtypeStruct((rank, columns), jnp.float32),
        ),
        in_specs=[
            pl.BlockSpec((rank, step), lambda i: (0, i)),
            pl.BlockSpec((rank, columns), lambda i: (0, 0)),
        ],
        out_specs=(
            pl.BlockSpec((step, columns), lambda i: (i, 0)),
            pl.BlockSpec((rank, step), lambda i: (0, i)),
            pl.BlockSpec((rank, columns), lambda i: (0, 0)),
        ),
        compiler_params=pltpu.CompilerParams(vmem_limit_bytes=16 * 2**20),
        name="powersgd_update",
    )(basis, coeff)
    return update, basis.T, coeff.T


def shards(axes, sizes, activations, out_grads, residual, right_prev):
    rows, columns = residual.shape
    rank = right_prev.shape[1]
    n_dp, n_tp = sizes["dp"], sizes["tp"]
    fits = (
        rank % ROWS == 0
        and 2 * rank <= LANES
        and min(n_dp, n_tp) > 1
        and n_dp % 2 == n_tp % 2 == 0
        and n_dp > 2
        and rows % (LANES * n_dp * n_tp) == 0
        and columns % (2 * LANES) == 0
        and (columns // LANES * (rank // ROWS)) % n_dp == 0
    )
    if not fits:
        return plain_shards(activations, out_grads, residual, right_prev)
    return fast_shards(axes, sizes, activations, out_grads, residual, right_prev)


def solution(mesh):
    in_specs = (P("dp", None), P("dp", "tp"), P("dp", "tp"), P("tp", None))
    out_specs = (P(None, "tp"), P(), P("tp", None))
    body = functools.partial(shards, mesh.axis_names, dict(mesh.shape))
    return jax.shard_map(body, mesh=mesh, in_specs=in_specs, out_specs=out_specs, check_vma=False)
```

```python
import functools
import itertools

import jax
import jax.numpy as jnp
from jax import lax
from jax.experimental import pallas as pl
from jax.experimental.pallas import tpu as pltpu
from jax.sharding import PartitionSpec as P

LANES = 128
ROWS = 8
HIGHEST = lax.Precision.HIGHEST


def plain_shards(activations, out_grads, residual, right_prev):
    product = lax.dot_general(
        activations, out_grads, (((0,), (0,)), ((), ())), preferred_element_type=jnp.float32
    )
    merged = (product + residual.astype(jnp.float32)).astype(jnp.bfloat16)
    shard_sum = lax.psum_scatter(
        jnp.dot(merged, right_prev, preferred_element_type=jnp.float32),
        "tp",
        scatter_dimension=0,
        tiled=True,
    )
    block_sum = lax.psum(shard_sum, "dp")
    block_gram = jnp.dot(block_sum.T, block_sum, precision=HIGHEST)
    gram_matrix = lax.psum(block_gram, "tp")
    lower_factor = jnp.linalg.cholesky(gram_matrix)
    basis_block = lax.linalg.triangular_solve(
        lower_factor, block_sum, left_side=False, lower=True, transpose_a=True
    )
    left_basis = lax.all_gather(basis_block, "tp", axis=0, tiled=True)
    left_half = left_basis.astype(jnp.bfloat16)
    coeff_terms = lax.dot_general(
        merged, left_half, (((0,), (0,)), ((), ())), preferred_element_type=jnp.float32
    )
    right_factor = lax.psum(coeff_terms, "dp") / lax.axis_size("dp")
    update = jnp.dot(left_basis, right_factor.T, precision=HIGHEST).astype(jnp.bfloat16)
    return (update, left_basis, right_factor)


def digits_of(axis, size):
    if size == 1:
        return []
    if size % 2 == 0 and size > 2:
        return [(axis, 1, 2), (axis, 2, size // 2)]
    return [(axis, 1, size)]


def members(stage):
    count = 1
    for _, _, size in stage:
        count *= size
    return count


def offsets(stage):
    return list(itertools.product(*[range(size) for _, _, size in stage]))[1:]


def member_index(stage, place):
    index = 0
    for axis, stride, size in stage:
        index = index * size + (place[axis] // stride) % size
    return index


def moved(stage, offset, place, sign=1):
    there = dict(place)
    for (axis, stride, size), step in zip(stage, offset):
        digit = (place[axis] // stride) % size
        there[axis] = there[axis] + (((digit + sign * step + size) % size) - digit) * stride
    return there


def split(value):
    high = value.astype(jnp.bfloat16)
    return high, (value - high.astype(jnp.float32)).astype(jnp.bfloat16)


def joined(units, rank):
    tall = rank // ROWS
    n = units.shape[0] // tall
    bands = [
        jnp.concatenate([units[b * tall + r] for b in range(n)], axis=1) for r in range(tall)
    ]
    return jnp.concatenate(bands, axis=0)


def round_kernel(
    left_stages, right_stages, n_chunk, axes,
    act, grads, resid, right_prev, basis_out, coeff_out,
    xbuf, ybuf, rbuf, merged, terms, acc2, full2, *rest,
):
    rest = list(rest)
    in_sem, send_sem, recv_sem = rest[-3:]
    take = iter(rest[:-3])
    acc, full = next(take), next(take)
    left_recv = [next(take) for _ in left_stages]
    right_recv = [next(take) for _ in right_stages]
    place = {axis: lax.axis_index(axis) for axis in axes}
    barrier = pltpu.get_barrier_semaphore()
    peers = {}
    for stage in left_stages + right_stages:
        for offset in offsets(stage):
            key = tuple(sorted((d, s) for d, s in zip(stage, offset) if s))
            peers[key] = moved(stage, offset, place)
    for peer in peers.values():
        pl.semaphore_signal(barrier, inc=1, device_id=peer, device_id_type=pl.DeviceIdType.MESH)

    rows, columns = resid.shape
    rank = right_prev.shape[0]
    tall = rank // ROWS
    chunk = rows // n_chunk
    per = chunk // LANES
    units = per * tall
    first, second = left_stages[:2]
    n0, n1 = members(first), members(second)
    order = []
    for offset in offsets(first) + [(0,) * len(first)]:
        for offset2 in offsets(second) + [(0,) * len(second)]:
            there = moved(second, offset2, moved(first, offset, place))
            order.append(member_index(first, there) * n1 + member_index(second, there))

    def x_copy(c):
        at = pl.multiple_of(c * chunk, chunk)
        return pltpu.make_async_copy(act.at[:, pl.ds(at, chunk)], xbuf.at[c], in_sem.at[c])

    def e_copy(c):
        at = pl.multiple_of(c * chunk, chunk)
        return pltpu.make_async_copy(
            resid.at[pl.ds(at, chunk), :], merged.at[pl.ds(at, chunk), :], in_sem.at[n_chunk + c]
        )

    y_copy = pltpu.make_async_copy(grads, ybuf, in_sem.at[2 * n_chunk])
    r_copy = pltpu.make_async_copy(right_prev, rbuf, in_sem.at[2 * n_chunk + 1])
    y_copy.start()
    r_copy.start()
    for c in order:
        x_copy(c).start()
        e_copy(c).start()
    y_copy.wait()
    r_copy.wait()

    slot = [0]
    sent = []

    def remote(src, dst, peer):
        n = slot[0]
        slot[0] += 1
        copy = pltpu.make_async_remote_copy(
            src_ref=src, dst_ref=dst, send_sem=send_sem.at[n], recv_sem=recv_sem.at[n],
            device_id=peer, device_id_type=pl.DeviceIdType.MESH,
        )
        copy.start()
        sent.append(copy)
        return copy

    def all_reduce(stages, acc_ref, recv_refs, full_ref, lo, count, held):
        for stage, recv in zip(stages, recv_refs):
            size = count // members(stage)
            copies = []
            for k, offset in enumerate(offsets(stage)):
                peer = moved(stage, offset, place)
                start = lo + member_index(stage, peer) * size
                copies.append(remote(acc_ref.at[pl.ds(start, size)], recv.at[k], peer))
            held = held + [(stage, lo, count)]
            lo, count = lo + member_index(stage, place) * size, size
            yield
            total = acc_ref[pl.ds(lo, count)]
            for k, copy in enumerate(copies):
                copy.wait_recv()
                total = total + recv[k]
            if stage is stages[-1]:
                full_ref[pl.ds(lo, count)] = total
            else:
                acc_ref[pl.ds(lo, count)] = total
        for stage, outer, outer_count in reversed(held):
            copies = []
            for offset in offsets(stage):
                peer = moved(stage, offset, place)
                mine = full_ref.at[pl.ds(lo, count)]
                copies.append(remote(mine, mine, peer))
            yield
            for copy in copies:
                copy.wait_recv()
            lo, count = outer, outer_count

    def advance(flow):
        return next(flow, "done") != "done"

    def merge(c):
        x_copy(c).wait()
        e_copy(c).wait()
        at = pl.multiple_of(c * chunk, chunk)
        product = lax.dot_general(
            xbuf[c], ybuf[...], (((0,), (0,)), ((), ())), preferred_element_type=jnp.float32
        )
        piece = (product + merged[pl.ds(at, chunk), :].astype(jnp.float32)).astype(jnp.bfloat16)
        merged[pl.ds(at, chunk), :] = piece
        term = lax.dot_general(
            rbuf[...], piece, (((1,), (1,)), ((), ())), preferred_element_type=jnp.float32
        )
        return [
            term[r * ROWS : (r + 1) * ROWS, b * LANES : (b + 1) * LANES]
            for b in range(per) for r in range(tall)
        ]

    arrivals = {}
    second_copies = []
    for n, c in enumerate(order):
        k0, k1 = divmod(n, n1)
        terms_of_chunk = merge(c)
        at = c * units
        if n == 0:
            pl.semaphore_wait(barrier, len(peers))
        if k0 < n0 - 1:
            for u, term in enumerate(terms_of_chunk):
                acc[at + u] = term
            peer = moved(first, offsets(first)[k0], place)
            arrivals[k0, k1] = remote(acc.at[pl.ds(at, units)], left_recv[0].at[k0, k1], peer)
            continue
        for j in range(n0 - 1):
            arrivals[j, k1].wait_recv()
        for u, term in enumerate(terms_of_chunk):
            for j in range(n0 - 1):
                term = term + left_recv[0][j, k1, u]
            acc[at + u] = term
        if k1 < n1 - 1:
            peer = moved(second, offsets(second)[k1], place)
            second_copies.append(remote(acc.at[pl.ds(at, units)], left_recv[1].at[k1], peer))
    mine = order[-1] * units
    total = acc[pl.ds(mine, units)]
    for k, copy in enumerate(second_copies):
        copy.wait_recv()
        total = total + left_recv[1][k]
    acc[pl.ds(mine, units)] = total

    tile = 2 * LANES
    span = rows // n0

    def add_terms(index, step):
        at = pl.multiple_of(index * span, span)
        both = jnp.concatenate(
            split(joined(full[pl.ds(index * n1 * units, n1 * units)], rank)), axis=0
        )

        def column_tile(j, carry):
            col = pl.multiple_of(j * tile, tile)
            part = jnp.dot(
                both, merged[pl.ds(at, span), pl.ds(col, tile)],
                preferred_element_type=jnp.float32,
            )
            part = part[:rank] + part[rank:]
            if step > 0:
                part = part + terms[:, pl.ds(col, tile)]
            if step < n0 - 1:
                terms[:, pl.ds(col, tile)] = part
            else:
                for b in range(2):
                    for r in range(tall):
                        acc2[(2 * j + b) * tall + r] = part[
                            r * ROWS : (r + 1) * ROWS, b * LANES : (b + 1) * LANES
                        ]
            return carry

        lax.fori_loop(0, columns // tile, column_tile, 0)

    flow = all_reduce(
        left_stages[2:], acc, left_recv[2:], full, mine, units,
        [(first, 0, n_chunk * units), (second, member_index(first, place) * n1 * units, n1 * units)],
    )
    for _ in range(2 * len(left_stages[2:]) + 2):
        advance(flow)
    add_terms(member_index(first, place), 0)
    while advance(flow):
        pass
    for k, offset in enumerate(offsets(first)):
        add_terms(member_index(first, moved(first, offset, place)), k + 1)

    right_flow = all_reduce(right_stages, acc2, right_recv, full2, 0, acc2.shape[0], [])
    advance(right_flow)
    left_sum = joined(full[...], rank)
    gram = lax.dot_general(
        left_sum, left_sum, (((1,), (1,)), ((), ())),
        precision=HIGHEST, preferred_element_type=jnp.float32,
    )
    row_id = lax.broadcasted_iota(jnp.int32, (rank, LANES), 0)
    col_id = lax.broadcasted_iota(jnp.int32, (rank, LANES), 1)
    work = jnp.concatenate(
        [gram, (row_id + rank == col_id).astype(jnp.float32)[:, rank:]], axis=1
    )
    for j in range(rank):
        column = jnp.broadcast_to(work[:, j : j + 1], (rank, LANES))
        scaled = work[j : j + 1, :] / column[j : j + 1, :]
        work = work - jnp.where(row_id > j, column, 0.0) * scaled
    pivots = jnp.sum(jnp.where(row_id == col_id, work, 0.0), axis=1, keepdims=True)
    inverse = work[:, rank : 2 * rank] / jnp.sqrt(pivots)
    advance(right_flow)
    basis_out[...] = jnp.dot(
        inverse, left_sum, precision=HIGHEST, preferred_element_type=jnp.float32
    )
    while advance(right_flow):
        pass
    coeff_out[...] = jnp.dot(
        inverse * (1.0 / lax.axis_size("dp")), joined(full2[...], rank),
        precision=HIGHEST, preferred_element_type=jnp.float32,
    )
    for copy in sent:
        copy.wait_send()


def update_kernel(basis, coeff, update_out, basis_out, coeff_out):
    left_high, left_low = split(basis[...])
    right_high, right_low = split(coeff[...])
    left = jnp.concatenate([left_high, left_low, left_high], axis=0)
    right = jnp.concatenate([right_high, right_high, right_low], axis=0)
    update_out[...] = lax.dot_general(
        left, right, (((0,), (0,)), ((), ())), preferred_element_type=jnp.float32
    ).astype(jnp.bfloat16)
    basis_out[...] = basis[...]
    coeff_out[...] = coeff[...]


def fast_shards(axes, sizes, activations, out_grads, residual, right_prev):
    rows, columns = residual.shape
    tokens = activations.shape[0]
    rank = right_prev.shape[1]
    n_dp, n_tp = sizes["dp"], sizes["tp"]
    tp_digits, dp_digits = digits_of("tp", n_tp), digits_of("dp", n_dp)
    left_stages = [s for s in (tp_digits[:1], tp_digits[1:] + dp_digits[:1], dp_digits[1:]) if s]
    right_stages = [dp_digits]
    n_first, n_second = members(left_stages[0]), members(left_stages[1])
    n_chunk = n_first * n_second
    tall = rank // ROWS
    units, units2 = rows // LANES * tall, columns // LANES * tall

    def unit_buffer(*lead):
        return pltpu.VMEM((*lead, ROWS, LANES), jnp.float32)

    def recv_buffers(stages, count):
        buffers = []
        for stage in stages:
            count //= members(stage)
            buffers.append(unit_buffer(members(stage) - 1, count))
        return buffers

    n_copies = 2 * sum(members(s) - 1 for s in right_stages + left_stages[1:])
    n_copies += (n_first - 1) * (n_second + 1)
    vmem = pl.BlockSpec(memory_space=pltpu.VMEM)
    hbm = pl.BlockSpec(memory_space=pltpu.HBM)
    basis, coeff = pl.pallas_call(
        functools.partial(round_kernel, left_stages, right_stages, n_chunk, axes),
        out_shape=(
            jax.ShapeDtypeStruct((rank, rows), jnp.float32),
            jax.ShapeDtypeStruct((rank, columns), jnp.float32),
        ),
        in_specs=[hbm, hbm, hbm, hbm],
        out_specs=(vmem, vmem),
        scratch_shapes=[
            pltpu.VMEM((n_chunk, tokens, rows // n_chunk), jnp.bfloat16),
            pltpu.VMEM((tokens, columns), jnp.bfloat16),
            pltpu.VMEM((rank, columns), jnp.bfloat16),
            pltpu.VMEM((rows, columns), jnp.bfloat16),
            pltpu.VMEM((rank, columns), jnp.float32),
            unit_buffer(units2),
            unit_buffer(units2),
            unit_buffer(units),
            unit_buffer(units),
            unit_buffer(n_first - 1, n_second, units // n_chunk),
            *recv_buffers(left_stages[1:], units // n_first),
            *recv_buffers(right_stages, units2),
            pltpu.SemaphoreType.DMA((2 * n_chunk + 2,)),
            pltpu.SemaphoreType.DMA((n_copies,)),
            pltpu.SemaphoreType.DMA((n_copies,)),
        ],
        compiler_params=pltpu.CompilerParams(
            collective_id=0, has_side_effects=True, vmem_limit_bytes=63 * 2**20 + 512 * 2**10
        ),
        name="powersgd_round",
    )(activations, out_grads, residual, right_prev.T)
    step = rows // 4
    update, basis, coeff = pl.pallas_call(
        update_kernel,
        grid=(rows // step,),
        out_shape=(
            jax.ShapeDtypeStruct((rows, columns), jnp.bfloat16),
            jax.ShapeDtypeStruct((rank, rows), jnp.float32),
            jax.ShapeDtypeStruct((rank, columns), jnp.float32),
        ),
        in_specs=[
            pl.BlockSpec((rank, step), lambda i: (0, i)),
            pl.BlockSpec((rank, columns), lambda i: (0, 0)),
        ],
        out_specs=(
            pl.BlockSpec((step, columns), lambda i: (i, 0)),
            pl.BlockSpec((rank, step), lambda i: (0, i)),
            pl.BlockSpec((rank, columns), lambda i: (0, 0)),
        ),
        compiler_params=pltpu.CompilerParams(vmem_limit_bytes=63 * 2**20 + 512 * 2**10),
        name="powersgd_update",
    )(basis, coeff)
    return update, basis.T, coeff.T


def shards(axes, sizes, activations, out_grads, residual, right_prev):
    rows, columns = residual.shape
    rank = right_prev.shape[1]
    n_dp, n_tp = sizes["dp"], sizes["tp"]
    fits = (
        rank % ROWS == 0
        and 2 * rank <= LANES
        and min(n_dp, n_tp) > 1
        and n_dp % 2 == n_tp % 2 == 0
        and n_dp > 2
        and rows % (LANES * n_dp * n_tp) == 0
        and columns % (2 * LANES) == 0
        and (columns // LANES * (rank // ROWS)) % n_dp == 0
    )
    if not fits:
        return plain_shards(activations, out_grads, residual, right_prev)
    return fast_shards(axes, sizes, activations, out_grads, residual, right_prev)


def solution(mesh):
    in_specs = (P("dp", None), P("dp", "tp"), P("dp", "tp"), P("tp", None))
    out_specs = (P(None, "tp"), P(), P("tp", None))
    body = functools.partial(shards, mesh.axis_names, dict(mesh.shape))
    return jax.shard_map(body, mesh=mesh, in_specs=in_specs, out_specs=out_specs, check_vma=False)
```
